512 devices in a mesh: row: 16 (over y, x_lo, core), col: 32 (over z, x_hi).
Axes of the slice: x: 4 (x_hi: 2, x_lo: 2; x = x_hi * 2 + x_lo), y: 4, z: 16, core: 2. Of those that a mesh axis runs over, the one named last changes fastest.
Arguments:
- traces: float32 [1024, 4096], P(('row', 'col')), may hold values from -6 to 6
- offsets: int32 [1024, 8], P(('row', 'col')), may hold values from 0 to 3072, as said below
- band_lo: int32 [1024], P(('row', 'col')), may hold values from 0 to 63
- band_hi: int32 [1024], P(('row', 'col')), may hold values from 192 to 256
- live: int32 [1024], P(('row', 'col')), may hold values 0 or 1
Outputs:
- correlations: bfloat16 [1024, 32, 16, 2, 512], P('row', 'col')
The draws below stay inside these ranges and needn't reach their ends.
Inputs may be any that keep to these rules, and one draw needn't show every extreme that they name: `offsets`: every offset is a multiple of 256.
All inputs are finite; a program needn't handle non-finite values. No bound on the sum of `live` on one device may be relied on, other than what follows from the above.
Results may differ from the reference program's by a relative error of at most 0.0052.
Values may be sent and summed in bfloat16 or wider, within the bound.
A program may use at most 64 MiB of HBM per device.

```python
import math
import jax
import jax.numpy as jnp
from jax import lax

CH_DEV = 2
SEG = 8
SAMPLES = 1024
BINS = 256
LAGS = 512
TRACE = 4096
CHANNELS = 1024
ROW_PANEL = 64
N_ROW = 16
N_COL = 32


def draw_offsets(key, part):
    quarter = SAMPLES // 4
    steps_count = (TRACE - SAMPLES) // quarter + 1
    return (quarter * jax.random.randint(key, (CHANNELS, SEG), 0, steps_count)).astype(jnp.int32)


def with_ends(drawn, own_key, least, high):
    longest = drawn.shape.index(max(drawn.shape))
    spots = []
    for shift in (0, 1):
        where = [jax.random.randint(jax.random.fold_in(own_key, axis), (), 0, length) for axis, length in enumerate(drawn.shape)]
        where[longest] = (where[longest] + shift) % drawn.shape[longest]
        spots.append(tuple(where))
    return drawn.at[spots[0]].set(least).at[spots[1]].set(high)


def level_of(stream_key, extent, split, least, high):
    level = 1.0
    for position, parts in split:
        heights = jax.random.uniform(jax.random.fold_in(jax.random.fold_in(stream_key, 6), position), (parts,), jnp.float32, least / len(split), high / len(split))
        level = level * jnp.repeat(jnp.exp(heights), extent[position] // parts).reshape((-1,) + (1,) * (len(extent) - 1 - position))
    return level


def normal_values(stream_key, extent, deviation, limit, cuts=(), kind=jnp.bfloat16):
    drawn = jax.random.normal(stream_key, extent, jnp.float32) * deviation
    if len(cuts) > 0:
        drawn = level_of(stream_key, extent, cuts, -0.22, 0.18) * drawn
    return jnp.clip(drawn, min=-limit, max=limit).astype(kind)


def setup_inputs(seed: int = 0) -> dict:
    key_of = jax.random.split(jax.random.key(seed), 6)
    traces = normal_values(key_of[0], (CHANNELS, TRACE), 1.0, 6.0, ((0, 512),), jnp.float32)
    offsets = draw_offsets(jax.random.fold_in(key_of[5], 71), 0)
    band_lo = with_ends(jax.random.randint(key_of[2], (CHANNELS,), 0, BINS // 4), jax.random.fold_in(key_of[2], 1), 0, (BINS // 4) - 1).astype(jnp.int32)
    band_hi = with_ends(jax.random.randint(key_of[3], (CHANNELS,), 3 * BINS // 4, BINS + 1), jax.random.fold_in(key_of[3], 1), 3 * BINS // 4, BINS).astype(jnp.int32)
    live = with_ends((jax.random.randint(key_of[4], (CHANNELS,), 0, 16) < 15).astype(jnp.int32), jax.random.fold_in(key_of[4], 1), 0, 1)
    return dict(traces=traces, offsets=offsets, band_lo=band_lo, band_hi=band_hi, live=live)


def transform_table():
    times = jnp.arange(SAMPLES, dtype=jnp.int32)
    freqs = jnp.arange(BINS, dtype=jnp.int32) + 1
    phase = jnp.mod(times[:, None] * freqs[None, :], SAMPLES).astype(jnp.float32) * (2.0 * math.pi / SAMPLES)
    taper = 0.5 - 0.5 * jnp.cos(times.astype(jnp.float32) * (2.0 * math.pi / SAMPLES))
    return jnp.concatenate([jnp.cos(phase), -jnp.sin(phase)], axis=1) * taper[:, None]

def lag_table():
    freqs = jnp.arange(BINS, dtype=jnp.int32) + 1
    shifts = jnp.arange(LAGS, dtype=jnp.int32) - LAGS // 2
    phase = jnp.mod(freqs[:, None] * shifts[None, :], SAMPLES).astype(jnp.float32) * (2.0 * math.pi / SAMPLES)
    return jnp.concatenate([jnp.cos(phase), -jnp.sin(phase)], axis=0) * (1.0 / math.sqrt(SEG * BINS))

def whiten(traces, offsets, band_lo, band_hi, live):

    def cut_one(record, start):
        return lax.dynamic_slice_in_dim(record, start, SAMPLES)

    def cut_channel(record, starts):
        return jax.vmap(cut_one, in_axes=(None, 0))(record, starts.astype(jnp.int32))
    segment = jax.vmap(cut_channel)(traces, offsets)
    count = traces.shape[0]
    flat = segment.reshape(count * SEG, SAMPLES)
    spec = jnp.dot(flat, transform_table(), precision=lax.Precision.HIGHEST)
    spec_re = spec[:, :BINS]
    spec_im = spec[:, BINS:]
    amp = jnp.sqrt(spec_re * spec_re + spec_im * spec_im)
    padded = jnp.pad(amp, ((0, 0), (2, 2)))
    smooth = (padded[:, 0:BINS] + padded[:, 1:BINS + 1] + padded[:, 2:BINS + 2] + padded[:, 3:BINS + 3] + padded[:, 4:BINS + 4]) / 5.0
    level = lax.optimization_barrier(jnp.mean(amp, axis=1, keepdims=True))
    factor = 1.0 / (smooth + 0.1 * level + 1e-06)
    bins = jnp.arange(BINS, dtype=jnp.int32)
    inside = (bins[None, :] >= band_lo[:, None]) & (bins[None, :] < band_hi[:, None]) & (live[:, None] == 1)
    keep = inside.astype(jnp.float32)
    factor = factor.reshape(count, SEG, BINS) * keep[:, None, :]
    spec = spec.reshape(count, SEG, 2 * BINS)
    white = spec * jnp.concatenate([factor, factor], axis=2)
    return white.astype(jnp.bfloat16)

def correlate(first, second, table):
    first = first.astype(jnp.float32)
    second = second.astype(jnp.float32)
    first_re, first_im = (first[..., :BINS], first[..., BINS:])
    second_re, second_im = (second[..., :BINS], second[..., BINS:])
    cross_re = jnp.einsum('isb,jsb->ijb', first_re, second_re) + jnp.einsum('isb,jsb->ijb', first_im, second_im)
    cross_im = jnp.einsum('isb,jsb->ijb', first_im, second_re) - jnp.einsum('isb,jsb->ijb', first_re, second_im)
    cross = jnp.concatenate([cross_re, cross_im], axis=2)
    count_i, count_j = (cross.shape[0], cross.shape[1])
    corr = jnp.dot(cross.reshape(count_i * count_j, 2 * BINS), table, precision=lax.Precision.HIGHEST)
    return corr.astype(jnp.bfloat16).reshape(count_i, count_j, LAGS)

def reference(traces, offsets, band_lo, band_hi, live):
    white = whiten(traces, offsets, band_lo, band_hi, live)
    columns = white.reshape(N_ROW, N_COL, CH_DEV, SEG, 2 * BINS).transpose(1, 0, 2, 3, 4).reshape(CHANNELS, SEG, 2 * BINS)
    panels = white.reshape(N_ROW, ROW_PANEL, SEG, 2 * BINS)
    table = lag_table()

    def one_panel(panel):
        return correlate(panel, columns, table)
    result = lax.map(one_panel, panels)
    return result.reshape(CHANNELS, N_COL, N_ROW, CH_DEV, LAGS)
```

```python
import functools
import math

import jax
import jax.numpy as jnp
import numpy as np
from jax import lax
from jax.experimental import pallas as pl
from jax.experimental.pallas import tpu as pltpu
from jax.sharding import PartitionSpec as P

SEG = 8
SAMPLES = 1024
QUARTER = SAMPLES // 4
BINS = 256
LAGS = 512
TRACE = 4096
CH_DEV = 2
ROWS = CH_DEV * SEG
MESH = pl.DeviceIdType.MESH

NZ, NY = 16, 4
N_ROW, N_COL = 16, 32
PANEL = N_COL * CH_DEV
SECOND = N_ROW * CH_DEV

GROUPS = (
    ((0, 0), (0, 1), (1, 0), (-1, 0)),
    ((1, 1), (-1, 1), (3, 0), (-3, 0)),
    ((6, 0), (-6, 0), (8, 0), (8, 1)),
    ((3, 1), (2, 0), (4, 0), (-3, 1)),
    ((-2, 0), (-4, 0), (2, 1), (4, 1)),
    ((-2, 1), (-4, 1), (6, 1), (-6, 1)),
    ((5, 0), (7, 0), (-5, 0), (-7, 0)),
    ((5, 1), (7, 1), (-5, 1), (-7, 1)),
)
SLOT = {d: n for n, d in enumerate(d for group in GROUPS for d in group)}
FAR = ((8, 1), (8, 0), (6, 0), (-6, 0), (3, 0), (-3, 0))
NEAR = ((1, 0), (-1, 0), (0, 1), (1, 1), (-1, 1))
RELAYED = ((3, 0), (-3, 0), (6, 0), (-6, 0))
COL_STEPS = tuple(dict.fromkeys(FAR + NEAR))
ROW_STEPS = tuple(
    (dy, dx, dc) for dy in (2, 1, -1, 0) for dx in (1, 0) for dc in (0, 1) if (dy, dx, dc) != (0, 0, 0)
)


def dft_table():
    times = np.arange(QUARTER)
    freqs = np.arange(BINS) + 1
    phase = (times[:, None] * freqs[None, :] % SAMPLES) * (2.0 * math.pi / SAMPLES)
    return np.concatenate([np.cos(phase), -np.sin(phase)], axis=1).astype(np.float32)


def taper_table():
    times = np.arange(SAMPLES)
    return (0.5 - 0.5 * np.cos(times * (2.0 * math.pi / SAMPLES))).reshape(4, QUARTER).astype(np.float32)


def lag_table():
    freqs = np.arange(BINS) + 1
    shifts = np.arange(LAGS) - LAGS // 2
    phase = np.mod(freqs[:, None] * shifts[None, :], SAMPLES) * (2.0 * math.pi / SAMPLES)
    return np.concatenate([np.cos(phase), -np.sin(phase)], axis=0).astype(np.float32)


def col_device(step, sign=1):
    col = lax.axis_index("col")
    z = lax.rem(col // 2 + sign * step[0] + 2 * NZ, NZ)
    x = lax.rem(col % 2 + step[1], 2)
    return {"col": z * 2 + x}


def row_device(step, sign=1):
    row = lax.axis_index("row")
    y = lax.rem(row // 4 + sign * step[0] + NY, NY)
    x = lax.rem((row // 2) % 2 + step[1], 2)
    core = lax.rem(row % 2 + step[2], 2)
    return {"row": (y * 2 + x) * 2 + core}


def whiten(traces, offsets, band_lo, band_hi, live, taper, dft, pieces):
    sub = lax.broadcasted_iota(jnp.int32, (SEG, BINS), 0)
    for k in range(CH_DEV):
        start = jnp.zeros((SEG, BINS), jnp.int32)
        for s in range(SEG):
            start = jnp.where(sub == s, offsets[k, s], start)
        cut = [jnp.zeros((SEG, QUARTER), jnp.float32) for _ in range(4)]
        for block in range(TRACE // QUARTER):
            samples = jnp.broadcast_to(
                traces[k : k + 1, block * QUARTER : (block + 1) * QUARTER], (SEG, QUARTER)
            )
            for q in range(4):
                place = block - q
                if 0 <= place <= TRACE // QUARTER - 4:
                    cut[q] = jnp.where(start == place * QUARTER, samples, cut[q])
        for q in range(4):
            row = q * ROWS + k * SEG
            pieces[row : row + SEG, :] = cut[q] * taper[q : q + 1, :]
    parts = jnp.dot(
        pieces[...], dft[...], precision=lax.Precision.HIGHEST, preferred_element_type=jnp.float32
    )
    lane = lax.broadcasted_iota(jnp.int32, (ROWS, BINS), 1)
    spec_re = parts[:ROWS, :BINS]
    spec_im = parts[:ROWS, BINS:]
    for q in range(1, 4):
        part_re = parts[q * ROWS : (q + 1) * ROWS, :BINS]
        part_im = parts[q * ROWS : (q + 1) * ROWS, BINS:]
        turn = ((lane + 1) * q) & 3
        spec_re = spec_re + jnp.where(
            turn == 0, part_re, jnp.where(turn == 1, part_im, jnp.where(turn == 2, -part_re, -part_im))
        )
        spec_im = spec_im + jnp.where(
            turn == 0, part_im, jnp.where(turn == 1, -part_re, jnp.where(turn == 2, -part_im, part_re))
        )
    amp = jnp.sqrt(spec_re * spec_re + spec_im * spec_im)

    def moved(by):
        return jnp.where((lane >= by) & (lane < BINS + by), pltpu.roll(amp, by % BINS, 1), 0.0)

    smooth = (moved(2) + moved(1) + amp + moved(-1) + moved(-2)) / 5.0
    level = jnp.sum(amp, axis=1, keepdims=True) * (1.0 / BINS)
    factor = 1.0 / (smooth + 0.1 * level + 1e-06)
    first = lax.broadcasted_iota(jnp.int32, (ROWS, BINS), 0) < SEG
    low = jnp.where(first, band_lo[0], band_lo[1])
    high = jnp.where(first, band_hi[0], band_hi[1])
    alive = jnp.where(first, live[0], live[1])
    inside = (lane >= low) & (lane < high) & (alive == 1)
    factor = factor * jnp.where(inside, 1.0, 0.0)
    return jnp.concatenate([spec_re * factor, spec_im * factor], axis=1).astype(jnp.bfloat16)


def kernel(
    offsets_in, band_lo_in, band_hi_in, live_in, traces_in, taper_in, dft_in, lags_in, out,
    offsets, band_lo, band_hi, live, traces, taper, dft, lags, load_sem, pieces, firsts, seconds, first_f32, second_f32, second_mix, cross,
    first_send, first_recv, second_send, second_recv,
):
    loads = [
        pltpu.make_async_copy(source, target, load_sem.at[n])
        for n, (source, target) in enumerate(
            (
                (traces_in, traces), (offsets_in, offsets), (band_lo_in, band_lo), (band_hi_in, band_hi),
                (live_in, live), (taper_in, taper), (dft_in, dft), (lags_in, lags),
            )
        )
    ]
    for load in loads:
        load.start()
    barrier = pltpu.get_barrier_semaphore()
    for step in COL_STEPS:
        pl.semaphore_signal(barrier, inc=1, device_id=col_device(step, -1), device_id_type=MESH)
    for step in ROW_STEPS:
        pl.semaphore_signal(barrier, inc=1, device_id=row_device(step, -1), device_id_type=MESH)

    for load in loads[:-1]:
        load.wait()
    white = whiten(traces, offsets, band_lo, band_hi, live, taper, dft, pieces)
    my_row = lax.axis_index("row")
    firsts[0] = white
    seconds[my_row] = white
    pl.semaphore_wait(barrier, len(COL_STEPS) + len(ROW_STEPS))

    def first_copy(held, step):
        slot = SLOT[(held[0] + step[0], (held[1] + step[1]) % 2)]
        return pltpu.make_async_remote_copy(
            src_ref=firsts.at[SLOT[held]],
            dst_ref=firsts.at[slot],
            send_sem=first_send.at[slot],
            recv_sem=first_recv.at[slot],
            device_id=col_device(step),
            device_id_type=MESH,
        )

    copies = {}
    for step in FAR + NEAR:
        copies[step] = first_copy((0, 0), step)
    second_copies = []
    for n, step in enumerate(ROW_STEPS):
        second_copies.append(
            pltpu.make_async_remote_copy(
                src_ref=firsts.at[0],
                dst_ref=seconds.at[my_row],
                send_sem=second_send.at[n],
                recv_sem=second_recv.at[n],
                device_id=row_device(step),
                device_id_type=MESH,
            )
        )
    for step in FAR:
        copies[step].start()
    for copy in second_copies:
        copy.start()
    for step in NEAR:
        copies[step].start()

    arrived = {(0, 0)}

    def take(place):
        if place not in arrived:
            arrived.add(place)
            copies[place].wait_recv()

    for place in RELAYED:
        take(place)
        for step in NEAR:
            copy = first_copy(place, step)
            copies[(place[0] + step[0], (place[1] + step[1]) % 2)] = copy
            copy.start()

    for copy in second_copies:
        copy.wait_recv()

    @pl.loop(0, N_ROW)
    def _(n):
        block = seconds[n].astype(jnp.float32) * (1.0 / math.sqrt(SEG * BINS))
        for tile in range(4):
            at = pl.ds(pl.multiple_of(n * ROWS, ROWS), ROWS)
            second_f32[tile, at, :] = block[:, tile * 128 : tile * 128 + 128]

    @pl.loop(0, SEG)
    def _(s):
        for tile in range(2):
            re = second_f32[tile, pl.ds(s, SECOND, stride=SEG), :]
            im = second_f32[2 + tile, pl.ds(s, SECOND, stride=SEG), :]
            second_mix[0, s, :, tile * 128 : tile * 128 + 128] = re
            second_mix[1, s, :, tile * 128 : tile * 128 + 128] = re - im
            second_mix[2, s, :, tile * 128 : tile * 128 + 128] = re + im

    loads[-1].wait()
    my_col = lax.axis_index("col")
    for g, group in enumerate(GROUPS):
        for place in group:
            take(place)

        @pl.loop(0, len(group))
        def _(t):
            block = firsts[g * 4 + t].astype(jnp.float32)
            for tile in range(4):
                first_f32[tile] = block[:, tile * 128 : tile * 128 + 128]
            for tile in range(2):
                first_f32[4 + tile] = (
                    block[:, tile * 128 : tile * 128 + 128] + block[:, BINS + tile * 128 : BINS + tile * 128 + 128]
                )
            for half in range(2):
                lo = half * 128
                total = [[[None] * 4 for _ in range(3)] for _ in range(CH_DEV)]
                for s in range(SEG):
                    b = [
                        [second_mix[m, s, jt * 8 : jt * 8 + 8, lo : lo + 128] for jt in range(4)]
                        for m in range(3)
                    ]
                    for k in range(CH_DEV):
                        row = k * SEG + s
                        a = [
                            first_f32[4 + half, pl.ds(row, 8, stride=0), :],
                            first_f32[2 + half, pl.ds(row, 8, stride=0), :],
                            first_f32[half, pl.ds(row, 8, stride=0), :],
                        ]
                        for m in range(3):
                            for jt in range(4):
                                term = a[m] * b[m][jt]
                                old = total[k][m][jt]
                                total[k][m][jt] = term if old is None else old + term
                for k in range(CH_DEV):
                    for pair in range(2):
                        re = [total[k][0][jt] - total[k][1][jt] for jt in (2 * pair, 2 * pair + 1)]
                        im = [total[k][0][jt] - total[k][2][jt] for jt in (2 * pair, 2 * pair + 1)]
                        at = pl.multiple_of(t * 64 + k * 32 + pair * 16, 16)
                        cross[pl.ds(at, 16), lo : lo + 128] = jnp.concatenate(re, 0).astype(jnp.bfloat16)
                        cross[pl.ds(at, 16), BINS + lo : BINS + lo + 128] = jnp.concatenate(im, 0).astype(
                            jnp.bfloat16
                        )

        corr = jnp.dot(cross[...], lags[...], preferred_element_type=jnp.float32).astype(jnp.bfloat16)
        for t, (dz, dx) in enumerate(group):
            source = lax.rem(my_col // 2 - dz + 2 * NZ, NZ) * 2 + lax.rem(my_col % 2 + dx, 2)
            out[pl.ds(source * 2, 2), 0] = corr[t * 64 : t * 64 + 64].reshape(2, N_ROW, CH_DEV, LAGS)

    for copy in copies.values():
        copy.wait_send()
    for copy in second_copies:
        copy.wait_send()


def body(traces, offsets, band_lo, band_hi, live):
    vmem = pl.BlockSpec(memory_space=pltpu.VMEM)
    hbm = pl.BlockSpec(memory_space=pltpu.HBM)
    stacked = pl.pallas_call(
        kernel,
        out_shape=jax.ShapeDtypeStruct((PANEL, 1, N_ROW, CH_DEV, LAGS), jnp.bfloat16),
        in_specs=[hbm] * 8,
        out_specs=vmem,
        scratch_shapes=[
            pltpu.SMEM((CH_DEV, SEG), jnp.int32),
            pltpu.SMEM((CH_DEV,), jnp.int32),
            pltpu.SMEM((CH_DEV,), jnp.int32),
            pltpu.SMEM((CH_DEV,), jnp.int32),
            pltpu.VMEM((CH_DEV, TRACE), jnp.float32),
            pltpu.VMEM((4, QUARTER), jnp.float32),
            pltpu.VMEM((QUARTER, 2 * BINS), jnp.float32),
            pltpu.VMEM((2 * BINS, LAGS), jnp.bfloat16),
            pltpu.SemaphoreType.DMA((8,)),
            pltpu.VMEM((4 * ROWS, QUARTER), jnp.float32),
            pltpu.VMEM((N_COL, ROWS, 2 * BINS), jnp.bfloat16),
            pltpu.VMEM((N_ROW, ROWS, 2 * BINS), jnp.bfloat16),
            pltpu.VMEM((6, ROWS, 128), jnp.float32),
            pltpu.VMEM((4, N_ROW * ROWS, 128), jnp.float32),
            pltpu.VMEM((3, SEG, SECOND, BINS), jnp.float32),
            pltpu.VMEM((256, 2 * BINS), jnp.bfloat16),
            pltpu.SemaphoreType.DMA((N_COL,)),
            pltpu.SemaphoreType.DMA((N_COL,)),
            pltpu.SemaphoreType.DMA((N_ROW,)),
            pltpu.SemaphoreType.DMA((N_ROW,)),
        ],
        compiler_params=pltpu.CompilerParams(collective_id=0, has_side_effects=True, vmem_limit_bytes=16 << 20),
        name="stack",
    )(
        *(
            pltpu.with_memory_space_constraint(operand, pltpu.HBM)
            for operand in (
                offsets, band_lo, band_hi, live, traces,
                jnp.asarray(taper_table()), jnp.asarray(dft_table()), jnp.asarray(lag_table(), jnp.bfloat16),
            )
        )
    )
    return stacked


def solution(mesh):
    in_specs = (
        P(("row", "col"), None),
        P(("row", "col"), None),
        P(("row", "col")),
        P(("row", "col")),
        P(("row", "col")),
    )
    out_specs = P("row", "col", None, None, None)
    return jax.shard_map(body, mesh=mesh, in_specs=in_specs, out_specs=out_specs, check_vma=False)
```

```python
import functools
import math

import jax
import jax.numpy as jnp
import numpy as np
from jax import lax
from jax.experimental import pallas as pl
from jax.experimental.pallas import tpu as pltpu
from jax.sharding import PartitionSpec as P

SEG = 8
SAMPLES = 1024
QUARTER = SAMPLES // 4
BINS = 256
LAGS = 512
TRACE = 4096
CH_DEV = 2
ROWS = CH_DEV * SEG
MESH = pl.DeviceIdType.MESH

NZ, NY = 16, 4
N_ROW, N_COL = 16, 32
PANEL = N_COL * CH_DEV
SECOND = N_ROW * CH_DEV
PAIRS = CH_DEV * SECOND

GROUPS = (
    ((0, 0), (1, 0), (-1, 0), (0, 1)),
    ((2, 0), (-2, 0), (1, 1), (-1, 1)),
    ((2, 1), (-2, 1), (5, 0), (-5, 0)),
    ((4, 0), (6, 0), (-4, 0), (-6, 0)),
    ((5, 1), (-5, 1), (3, 0), (-3, 0)),
    ((7, 0), (-7, 0), (4, 1), (6, 1)),
    ((-4, 1), (-6, 1), (8, 0), (3, 1)),
    ((-3, 1), (7, 1), (-7, 1), (8, 1)),
)
PLACES = tuple(d for group in GROUPS for d in group)
SLOT = {d: n for n, d in enumerate(PLACES)}
FAR = ((5, 0), (-5, 0))
NEAR = ((2, 1), (-2, 1), (1, 1), (-1, 1), (2, 0), (-2, 0), (0, 1), (1, 0), (-1, 0))
RELAYS = {(5, 0): ((3, 1), (3, 0)) + NEAR, (-5, 0): NEAR}
COL_STEPS = FAR + NEAR + ((3, 0), (3, 1))
ROW_STEPS = tuple(
    (dy, dx, dc) for dy in (2, 1, -1, 0) for dx in (1, 0) for dc in (0, 1) if (dy, dx, dc) != (0, 0, 0)
)


def dft_table():
    times = np.arange(QUARTER)
    freqs = np.arange(BINS) + 1
    phase = (times[:, None] * freqs[None, :] % SAMPLES) * (2.0 * math.pi / SAMPLES)
    return np.concatenate([np.cos(phase), -np.sin(phase)], axis=1).astype(np.float32)


def taper_table():
    times = np.arange(SAMPLES)
    return (0.5 - 0.5 * np.cos(times * (2.0 * math.pi / SAMPLES))).reshape(4, QUARTER).astype(np.float32)


def lag_table():
    freqs = np.arange(BINS) + 1
    shifts = np.arange(LAGS) - LAGS // 2
    phase = np.mod(freqs[:, None] * shifts[None, :], SAMPLES) * (2.0 * math.pi / SAMPLES)
    return np.concatenate([np.cos(phase), -np.sin(phase)], axis=0).astype(np.float32)


def col_device(step, sign=1):
    col = lax.axis_index("col")
    z = lax.rem(col // 2 + sign * step[0] + 2 * NZ, NZ)
    x = lax.rem(col % 2 + step[1], 2)
    return {"col": z * 2 + x}


def row_device(step, sign=1):
    row = lax.axis_index("row")
    y = lax.rem(row // 4 + sign * step[0] + NY, NY)
    x = lax.rem((row // 2) % 2 + step[1], 2)
    core = lax.rem(row % 2 + step[2], 2)
    return {"row": (y * 2 + x) * 2 + core}


def whiten(traces, offsets, band_lo, band_hi, live, taper, dft, pieces, dft_load):
    sub = lax.broadcasted_iota(jnp.int32, (SEG, BINS), 0)
    for k in range(CH_DEV):
        start = jnp.zeros((SEG, BINS), jnp.int32)
        for s in range(SEG):
            start = jnp.where(sub == s, offsets[k, s], start)
        cut = [jnp.zeros((SEG, QUARTER), jnp.float32) for _ in range(4)]
        for block in range(TRACE // QUARTER):
            samples = jnp.broadcast_to(
                traces[k : k + 1, block * QUARTER : (block + 1) * QUARTER], (SEG, QUARTER)
            )
            for q in range(4):
                place = block - q
                if 0 <= place <= TRACE // QUARTER - 4:
                    cut[q] = jnp.where(start == place * QUARTER, samples, cut[q])
        for q in range(4):
            row = q * ROWS + k * SEG
            pieces[row : row + SEG, :] = cut[q] * taper[q : q + 1, :]
    dft_load.wait()
    parts = jnp.dot(
        pieces[...], dft[...], precision=lax.Precision.HIGHEST, preferred_element_type=jnp.float32
    )
    lane = lax.broadcasted_iota(jnp.int32, (ROWS, BINS), 1)
    spec_re = parts[:ROWS, :BINS]
    spec_im = parts[:ROWS, BINS:]
    for q in range(1, 4):
        part_re = parts[q * ROWS : (q + 1) * ROWS, :BINS]
        part_im = parts[q * ROWS : (q + 1) * ROWS, BINS:]
        turn = ((lane + 1) * q) & 3
        spec_re = spec_re + jnp.where(
            turn == 0, part_re, jnp.where(turn == 1, part_im, jnp.where(turn == 2, -part_re, -part_im))
        )
        spec_im = spec_im + jnp.where(
            turn == 0, part_im, jnp.where(turn == 1, -part_re, jnp.where(turn == 2, -part_im, part_re))
        )
    amp = jnp.sqrt(spec_re * spec_re + spec_im * spec_im)

    def moved(by):
        return jnp.where((lane >= by) & (lane < BINS + by), pltpu.roll(amp, by % BINS, 1), 0.0)

    smooth = (moved(2) + moved(1) + amp + moved(-1) + moved(-2)) / 5.0
    level = jnp.sum(amp, axis=1, keepdims=True) * (1.0 / BINS)
    factor = 1.0 / (smooth + 0.1 * level + 1e-06)
    first = lax.broadcasted_iota(jnp.int32, (ROWS, BINS), 0) < SEG
    low = jnp.where(first, band_lo[0], band_lo[1])
    high = jnp.where(first, band_hi[0], band_hi[1])
    alive = jnp.where(first, live[0], live[1])
    inside = (lane >= low) & (lane < high) & (alive == 1)
    factor = factor * jnp.where(inside, 1.0, 0.0)
    return jnp.concatenate([spec_re * factor, spec_im * factor], axis=1).astype(jnp.bfloat16)


def kernel(
    offsets_in, band_lo_in, band_hi_in, live_in, traces_in, taper_in, dft_in, lags_in, out,
    offsets, band_lo, band_hi, live, traces, taper, dft, lags, load_sem, pieces, firsts, seconds, first_f32, second_mix, cross_a, cross_b,
    first_send, first_recv, second_send, second_recv,
):
    loads = [
        pltpu.make_async_copy(source, target, load_sem.at[n])
        for n, (source, target) in enumerate(
            (
                (traces_in, traces), (offsets_in, offsets), (band_lo_in, band_lo), (band_hi_in, band_hi),
                (live_in, live), (taper_in, taper), (dft_in, dft), (lags_in, lags),
            )
        )
    ]
    for load in loads:
        load.start()
    barrier = pltpu.get_barrier_semaphore()
    for step in COL_STEPS:
        pl.semaphore_signal(barrier, inc=1, device_id=col_device(step, -1), device_id_type=MESH)
    for step in ROW_STEPS:
        pl.semaphore_signal(barrier, inc=1, device_id=row_device(step, -1), device_id_type=MESH)

    for load in loads[:-2]:
        load.wait()
    white = whiten(traces, offsets, band_lo, band_hi, live, taper, dft, pieces, loads[-2])
    my_row = lax.axis_index("row")
    firsts[0] = white
    seconds[my_row] = white
    pl.semaphore_wait(barrier, len(COL_STEPS) + len(ROW_STEPS))

    def first_copy(held, step):
        slot = SLOT[(held[0] + step[0], (held[1] + step[1]) % 2)]
        return pltpu.make_async_remote_copy(
            src_ref=firsts.at[SLOT[held]],
            dst_ref=firsts.at[slot],
            send_sem=first_send.at[slot],
            recv_sem=first_recv.at[slot],
            device_id=col_device(step),
            device_id_type=MESH,
        )

    copies = {}
    for step in FAR + NEAR:
        copies[step] = first_copy((0, 0), step)
    second_copies = []
    for n, step in enumerate(ROW_STEPS):
        second_copies.append(
            pltpu.make_async_remote_copy(
                src_ref=firsts.at[0],
                dst_ref=seconds.at[my_row],
                send_sem=second_send.at[n],
                recv_sem=second_recv.at[n],
                device_id=row_device(step),
                device_id_type=MESH,
            )
        )
    for step in FAR:
        copies[step].start()
    for copy in second_copies:
        copy.start()
    for step in NEAR:
        copies[step].start()

    arrived = {(0, 0)}

    def take(place):
        if place not in arrived:
            arrived.add(place)
            copies[place].wait_recv()

    for place, steps in RELAYS.items():
        take(place)
        for step in steps:
            copy = first_copy(place, step)
            copies[(place[0] + step[0], (place[1] + step[1]) % 2)] = copy
            copy.start()

    for copy in second_copies:
        copy.wait_recv()

    @pl.loop(0, N_ROW)
    def _(n):
        block = seconds[n].astype(jnp.float32) * (1.0 / math.sqrt(SEG * BINS))
        for k in range(CH_DEV):
            for tile in range(2):
                re = block[k * SEG : k * SEG + SEG, tile * 128 : tile * 128 + 128]
                im = block[k * SEG : k * SEG + SEG, BINS + tile * 128 : BINS + tile * 128 + 128]
                at = pl.ds(n * 2 + k, SEG, stride=SECOND)
                for m, mixed in enumerate((re, re - im, re + im)):
                    second_mix[2 * m + tile, at, :] = mixed

    loads[-1].wait()
    my_col = lax.axis_index("col")

    def source_of(place):
        return lax.rem(my_col // 2 - place[0] + 2 * NZ, NZ) * 2 + lax.rem(my_col % 2 + place[1], 2)

    crosses = (cross_a, cross_b)

    def cross_block(n, v, buffer, base):
        block = firsts[n].astype(jnp.float32)
        for tile in range(4):
            first_f32[6 * v + tile] = block[:, tile * 128 : tile * 128 + 128]
        for tile in range(2):
            lo = tile * 128
            first_f32[6 * v + 4 + tile] = block[:, lo : lo + 128] + block[:, BINS + lo : BINS + lo + 128]
        for half in range(2):
            lo = half * 128
            total = [[[None] * 4 for _ in range(3)] for _ in range(CH_DEV)]
            for s in range(SEG):
                b = [
                    [second_mix[2 * m + half, s * SECOND + jt * 8 : s * SECOND + jt * 8 + 8, :] for jt in range(4)]
                    for m in range(3)
                ]
                for k in range(CH_DEV):
                    row = k * SEG + s
                    a = [first_f32[6 * v + tile + half, pl.ds(row, 8, stride=0), :] for tile in (4, 2, 0)]
                    for m in range(3):
                        for jt in range(4):
                            term = a[m] * b[m][jt]
                            old = total[k][m][jt]
                            total[k][m][jt] = term if old is None else old + term
            for k in range(CH_DEV):
                for pair in range(2):
                    tiles = (2 * pair, 2 * pair + 1)
                    re = [total[k][0][jt] - total[k][1][jt] for jt in tiles]
                    im = [total[k][0][jt] - total[k][2][jt] for jt in tiles]
                    at = pl.ds(pl.multiple_of(base + k * SECOND + pair * 16, 16), 16)
                    buffer[at, lo : lo + 128] = jnp.concatenate(re, 0).astype(jnp.bfloat16)
                    buffer[at, BINS + lo : BINS + lo + 128] = jnp.concatenate(im, 0).astype(jnp.bfloat16)

    def lag_half(g, u):
        at = pl.ds(pl.multiple_of(u * 256, 256), 256)
        corr = jnp.dot(crosses[g % 2][...], lags[:, at], preferred_element_type=jnp.float32)
        corr = corr.astype(jnp.bfloat16)
        for t, place in enumerate(GROUPS[g]):
            rows = corr[t * PAIRS : (t + 1) * PAIRS].reshape(CH_DEV, N_ROW, CH_DEV, 256)
            out[pl.ds(source_of(place) * 2, 2), 0, :, :, at] = rows

    def step(g, u):
        if g > 0:
            lag_half(g - 1, u)
        for v in range(2):
            t = 2 * u + v
            cross_block(g * 4 + t, v, crosses[g % 2], t * PAIRS)

    for g, group in enumerate(GROUPS):
        if g < len(GROUPS) - 2:
            for place in group:
                take(place)

            @pl.loop(0, 2)
            def _(u):
                step(g, u)
        else:
            for u in range(2):
                take(group[2 * u])
                take(group[2 * u + 1])
                step(g, u)
    for u in range(2):
        lag_half(len(GROUPS) - 1, u)

    for copy in copies.values():
        copy.wait_send()
    for copy in second_copies:
        copy.wait_send()


def body(traces, offsets, band_lo, band_hi, live):
    vmem = pl.BlockSpec(memory_space=pltpu.VMEM)
    hbm = pl.BlockSpec(memory_space=pltpu.HBM)
    stacked = pl.pallas_call(
        kernel,
        out_shape=jax.ShapeDtypeStruct((PANEL, 1, N_ROW, CH_DEV, LAGS), jnp.bfloat16),
        in_specs=[hbm] * 8,
        out_specs=vmem,
        scratch_shapes=[
            pltpu.SMEM((CH_DEV, SEG), jnp.int32),
            pltpu.SMEM((CH_DEV,), jnp.int32),
            pltpu.SMEM((CH_DEV,), jnp.int32),
            pltpu.SMEM((CH_DEV,), jnp.int32),
            pltpu.VMEM((CH_DEV, TRACE), jnp.float32),
            pltpu.VMEM((4, QUARTER), jnp.float32),
            pltpu.VMEM((QUARTER, 2 * BINS), jnp.float32),
            pltpu.VMEM((2 * BINS, LAGS), jnp.bfloat16),
            pltpu.SemaphoreType.DMA((8,)),
            pltpu.VMEM((4 * ROWS, QUARTER), jnp.float32),
            pltpu.VMEM((N_COL, ROWS, 2 * BINS), jnp.bfloat16),
            pltpu.VMEM((N_ROW, ROWS, 2 * BINS), jnp.bfloat16),
            pltpu.VMEM((12, ROWS, 128), jnp.float32),
            pltpu.VMEM((6, SEG * SECOND, 128), jnp.float32),
            pltpu.VMEM((4 * PAIRS, 2 * BINS), jnp.bfloat16),
            pltpu.VMEM((4 * PAIRS, 2 * BINS), jnp.bfloat16),
            pltpu.SemaphoreType.DMA((N_COL,)),
            pltpu.SemaphoreType.DMA((N_COL,)),
            pltpu.SemaphoreType.DMA((N_ROW,)),
            pltpu.SemaphoreType.DMA((N_ROW,)),
        ],
        compiler_params=pltpu.CompilerParams(collective_id=0, has_side_effects=True, vmem_limit_bytes=16 << 20),
        name="stack",
    )(
        *(
            pltpu.with_memory_space_constraint(operand, pltpu.HBM)
            for operand in (
                offsets, band_lo, band_hi, live, traces,
                jnp.asarray(taper_table()), jnp.asarray(dft_table()), jnp.asarray(lag_table(), jnp.bfloat16),
            )
        )
    )
    return stacked


def solution(mesh):
    in_specs = (
        P(("row", "col"), None),
        P(("row", "col"), None),
        P(("row", "col")),
        P(("row", "col")),
        P(("row", "col")),
    )
    out_specs = P("row", "col", None, None, None)
    return jax.shard_map(body, mesh=mesh, in_specs=in_specs, out_specs=out_specs, check_vma=False)
```

```python
import functools
import math

import jax
import jax.numpy as jnp
import numpy as np
from jax import lax
from jax.experimental import pallas as pl
from jax.experimental.pallas import tpu as pltpu
from jax.sharding import PartitionSpec as P

SEG = 8
SAMPLES = 1024
QUARTER = SAMPLES // 4
BINS = 256
LAGS = 512
TRACE = 4096
CH_DEV = 2
ROWS = CH_DEV * SEG
MESH = pl.DeviceIdType.MESH

NZ, NY = 16, 4
N_ROW, N_COL = 16, 32
PANEL = N_COL * CH_DEV
SECOND = N_ROW * CH_DEV
PAIRS = CH_DEV * SECOND

GROUPS = (
    ((0, 0), (1, 0), (-1, 0), (0, 1)),
    ((2, 0), (-2, 0), (1, 1), (-1, 1)),
    ((2, 1), (-2, 1), (5, 0), (-5, 0)),
    ((4, 0), (6, 0), (-4, 0), (-6, 0)),
    ((5, 1), (-5, 1), (3, 0), (-3, 0)),
    ((7, 0), (-7, 0), (4, 1), (6, 1)),
    ((-4, 1), (-6, 1), (8, 0), (3, 1)),
    ((-3, 1), (7, 1), (-7, 1), (8, 1)),
)
PLACES = tuple(d for group in GROUPS for d in group)
SLOT = {d: n for n, d in enumerate(PLACES)}
FAR = ((5, 0), (-5, 0))
NEAR = ((1, 0), (-1, 0), (2, 0), (-2, 0), (0, 1), (1, 1), (-1, 1), (2, 1), (-2, 1))
RELAYS = {(5, 0): NEAR[:4] + ((3, 0),) + NEAR[4:] + ((3, 1),), (-5, 0): NEAR}
COL_STEPS = FAR + NEAR + ((3, 0), (3, 1))
ROW_STEPS = tuple(
    (dy, dx, dc) for dy in (2, 1, -1, 0) for dx in (1, 0) for dc in (0, 1) if (dy, dx, dc) != (0, 0, 0)
)


def dft_table():
    times = np.arange(QUARTER)
    freqs = np.arange(BINS) + 1
    phase = (times[:, None] * freqs[None, :] % SAMPLES) * (2.0 * math.pi / SAMPLES)
    return np.concatenate([np.cos(phase), -np.sin(phase)], axis=1).astype(np.float32)


def taper_table():
    times = np.arange(SAMPLES)
    return (0.5 - 0.5 * np.cos(times * (2.0 * math.pi / SAMPLES))).reshape(4, QUARTER).astype(np.float32)


def lag_table():
    freqs = np.arange(BINS) + 1
    shifts = np.arange(LAGS) - LAGS // 2
    phase = np.mod(freqs[:, None] * shifts[None, :], SAMPLES) * (2.0 * math.pi / SAMPLES)
    return np.concatenate([np.cos(phase), -np.sin(phase)], axis=0).astype(np.float32)


def col_device(step, sign=1):
    col = lax.axis_index("col")
    z = lax.rem(col // 2 + sign * step[0] + 2 * NZ, NZ)
    x = lax.rem(col % 2 + step[1], 2)
    return {"col": z * 2 + x}


def row_device(step, sign=1):
    row = lax.axis_index("row")
    y = lax.rem(row // 4 + sign * step[0] + NY, NY)
    x = lax.rem((row // 2) % 2 + step[1], 2)
    core = lax.rem(row % 2 + step[2], 2)
    return {"row": (y * 2 + x) * 2 + core}


def whiten(traces, offsets, band_lo, band_hi, live, taper, dft, pieces, dft_load):
    sub = lax.broadcasted_iota(jnp.int32, (SEG, BINS), 0)
    for k in range(CH_DEV):
        start = jnp.zeros((SEG, BINS), jnp.int32)
        for s in range(SEG):
            start = jnp.where(sub == s, offsets[k, s], start)
        cut = [jnp.zeros((SEG, QUARTER), jnp.float32) for _ in range(4)]
        for block in range(TRACE // QUARTER):
            samples = jnp.broadcast_to(
                traces[k : k + 1, block * QUARTER : (block + 1) * QUARTER], (SEG, QUARTER)
            )
            for q in range(4):
                place = block - q
                if 0 <= place <= TRACE // QUARTER - 4:
                    cut[q] = jnp.where(start == place * QUARTER, samples, cut[q])
        for q in range(4):
            row = q * ROWS + k * SEG
            pieces[row : row + SEG, :] = cut[q] * taper[q : q + 1, :]
    dft_load.wait()
    parts = jnp.dot(
        pieces[...], dft[...], precision=lax.Precision.HIGHEST, preferred_element_type=jnp.float32
    )
    lane = lax.broadcasted_iota(jnp.int32, (ROWS, BINS), 1)
    spec_re = parts[:ROWS, :BINS]
    spec_im = parts[:ROWS, BINS:]
    for q in range(1, 4):
        part_re = parts[q * ROWS : (q + 1) * ROWS, :BINS]
        part_im = parts[q * ROWS : (q + 1) * ROWS, BINS:]
        turn = ((lane + 1) * q) & 3
        spec_re = spec_re + jnp.where(
            turn == 0, part_re, jnp.where(turn == 1, part_im, jnp.where(turn == 2, -part_re, -part_im))
        )
        spec_im = spec_im + jnp.where(
            turn == 0, part_im, jnp.where(turn == 1, -part_re, jnp.where(turn == 2, -part_im, part_re))
        )
    amp = jnp.sqrt(spec_re * spec_re + spec_im * spec_im)

    def moved(by):
        return jnp.where((lane >= by) & (lane < BINS + by), pltpu.roll(amp, by % BINS, 1), 0.0)

    smooth = (moved(2) + moved(1) + amp + moved(-1) + moved(-2)) / 5.0
    level = jnp.sum(amp, axis=1, keepdims=True) * (1.0 / BINS)
    factor = 1.0 / (smooth + 0.1 * level + 1e-06)
    first = lax.broadcasted_iota(jnp.int32, (ROWS, BINS), 0) < SEG
    low = jnp.where(first, band_lo[0], band_lo[1])
    high = jnp.where(first, band_hi[0], band_hi[1])
    alive = jnp.where(first, live[0], live[1])
    inside = (lane >= low) & (lane < high) & (alive == 1)
    factor = factor * jnp.where(inside, 1.0, 0.0)
    return jnp.concatenate([spec_re * factor, spec_im * factor], axis=1).astype(jnp.bfloat16)


def kernel(
    offsets_in, band_lo_in, band_hi_in, live_in, traces_in, taper_in, dft_in, lags_in, out,
    offsets, band_lo, band_hi, live, traces, taper, dft, lags, load_sem, pieces, firsts, seconds, first_f32, second_mix, cross_a, cross_b,
    first_send, first_recv, second_send, second_recv,
):
    loads = [
        pltpu.make_async_copy(source, target, load_sem.at[n])
        for n, (source, target) in enumerate(
            (
                (traces_in, traces), (offsets_in, offsets), (band_lo_in, band_lo), (band_hi_in, band_hi),
                (live_in, live), (taper_in, taper), (dft_in, dft), (lags_in, lags),
            )
        )
    ]
    for load in loads:
        load.start()
    barrier = pltpu.get_barrier_semaphore()
    for step in COL_STEPS:
        pl.semaphore_signal(barrier, inc=1, device_id=col_device(step, -1), device_id_type=MESH)
    for step in ROW_STEPS:
        pl.semaphore_signal(barrier, inc=1, device_id=row_device(step, -1), device_id_type=MESH)

    for load in loads[:-2]:
        load.wait()
    white = whiten(traces, offsets, band_lo, band_hi, live, taper, dft, pieces, loads[-2])
    my_row = lax.axis_index("row")
    firsts[0] = white
    seconds[my_row] = white
    pl.semaphore_wait(barrier, len(COL_STEPS) + len(ROW_STEPS))

    def first_copy(held, step):
        slot = SLOT[(held[0] + step[0], (held[1] + step[1]) % 2)]
        return pltpu.make_async_remote_copy(
            src_ref=firsts.at[SLOT[held]],
            dst_ref=firsts.at[slot],
            send_sem=first_send.at[slot],
            recv_sem=first_recv.at[slot],
            device_id=col_device(step),
            device_id_type=MESH,
        )

    copies = {}
    for step in FAR + NEAR:
        copies[step] = first_copy((0, 0), step)
    second_copies = []
    for n, step in enumerate(ROW_STEPS):
        second_copies.append(
            pltpu.make_async_remote_copy(
                src_ref=firsts.at[0],
                dst_ref=seconds.at[my_row],
                send_sem=second_send.at[n],
                recv_sem=second_recv.at[n],
                device_id=row_device(step),
                device_id_type=MESH,
            )
        )
    for step in FAR:
        copies[step].start()
    for copy in second_copies:
        copy.start()
    for step in NEAR:
        copies[step].start()

    arrived = {(0, 0)}

    def take(place):
        if place not in arrived:
            arrived.add(place)
            copies[place].wait_recv()

    for place, steps in RELAYS.items():
        take(place)
        for step in steps:
            copy = first_copy(place, step)
            copies[(place[0] + step[0], (place[1] + step[1]) % 2)] = copy
            copy.start()

    def mix(row):
        block = seconds[row].astype(jnp.float32) * (1.0 / math.sqrt(SEG * BINS))
        for k in range(CH_DEV):
            for tile in range(2):
                re = block[k * SEG : k * SEG + SEG, tile * 128 : tile * 128 + 128]
                im = block[k * SEG : k * SEG + SEG, BINS + tile * 128 : BINS + tile * 128 + 128]
                at = pl.ds(row * 2 + k, SEG, stride=SECOND)
                for m, mixed in enumerate((re, re - im, re + im)):
                    second_mix[2 * m + tile, at, :] = mixed

    mix(my_row)
    for n in range(len(ROW_STEPS) - 1, -1, -1):
        second_copies[n].wait_recv()
        mix(row_device(ROW_STEPS[n], -1)["row"])

    loads[-1].wait()
    my_col = lax.axis_index("col")

    def source_of(place):
        return lax.rem(my_col // 2 - place[0] + 2 * NZ, NZ) * 2 + lax.rem(my_col % 2 + place[1], 2)

    crosses = (cross_a, cross_b)

    def cross_block(n, v, buffer, base):
        block = firsts[n].astype(jnp.float32)
        for tile in range(4):
            first_f32[6 * v + tile] = block[:, tile * 128 : tile * 128 + 128]
        for tile in range(2):
            lo = tile * 128
            first_f32[6 * v + 4 + tile] = block[:, lo : lo + 128] + block[:, BINS + lo : BINS + lo + 128]
        for half in range(2):
            lo = half * 128
            total = [[[None] * 4 for _ in range(3)] for _ in range(CH_DEV)]
            for s in range(SEG):
                b = [
                    [second_mix[2 * m + half, s * SECOND + jt * 8 : s * SECOND + jt * 8 + 8, :] for jt in range(4)]
                    for m in range(3)
                ]
                for k in range(CH_DEV):
                    row = k * SEG + s
                    a = [first_f32[6 * v + tile + half, pl.ds(row, 8, stride=0), :] for tile in (4, 2, 0)]
                    for m in range(3):
                        for jt in range(4):
                            term = a[m] * b[m][jt]
                            old = total[k][m][jt]
                            total[k][m][jt] = term if old is None else old + term
            for k in range(CH_DEV):
                for pair in range(2):
                    tiles = (2 * pair, 2 * pair + 1)
                    re = [total[k][0][jt] - total[k][1][jt] for jt in tiles]
                    im = [total[k][0][jt] - total[k][2][jt] for jt in tiles]
                    at = pl.ds(pl.multiple_of(base + k * SECOND + pair * 16, 16), 16)
                    buffer[at, lo : lo + 128] = jnp.concatenate(re, 0).astype(jnp.bfloat16)
                    buffer[at, BINS + lo : BINS + lo + 128] = jnp.concatenate(im, 0).astype(jnp.bfloat16)

    def lag_half(g, u):
        at = pl.ds(pl.multiple_of(u * 256, 256), 256)
        corr = jnp.dot(crosses[g % 2][...], lags[:, at], preferred_element_type=jnp.float32)
        corr = corr.astype(jnp.bfloat16)
        for t, place in enumerate(GROUPS[g]):
            rows = corr[t * PAIRS : (t + 1) * PAIRS].reshape(CH_DEV, N_ROW, CH_DEV, 256)
            out[pl.ds(source_of(place) * 2, 2), 0, :, :, at] = rows

    def step(g, u):
        if g > 0:
            lag_half(g - 1, u)
        for v in range(2):
            t = 2 * u + v
            cross_block(g * 4 + t, v, crosses[g % 2], t * PAIRS)

    for g, group in enumerate(GROUPS):
        if g < len(GROUPS) - 2:
            for place in group:
                take(place)

            @pl.loop(0, 2)
            def _(u):
                step(g, u)
        else:
            for u in range(2):
                take(group[2 * u])
                take(group[2 * u + 1])
                step(g, u)
    for u in range(2):
        lag_half(len(GROUPS) - 1, u)

    for copy in copies.values():
        copy.wait_send()
    for copy in second_copies:
        copy.wait_send()


def body(traces, offsets, band_lo, band_hi, live):
    vmem = pl.BlockSpec(memory_space=pltpu.VMEM)
    hbm = pl.BlockSpec(memory_space=pltpu.HBM)
    stacked = pl.pallas_call(
        kernel,
        out_shape=jax.ShapeDtypeStruct((PANEL, 1, N_ROW, CH_DEV, LAGS), jnp.bfloat16),
        in_specs=[hbm] * 8,
        out_specs=vmem,
        scratch_shapes=[
            pltpu.SMEM((CH_DEV, SEG), jnp.int32),
            pltpu.SMEM((CH_DEV,), jnp.int32),
            pltpu.SMEM((CH_DEV,), jnp.int32),
            pltpu.SMEM((CH_DEV,), jnp.int32),
            pltpu.VMEM((CH_DEV, TRACE), jnp.float32),
            pltpu.VMEM((4, QUARTER), jnp.float32),
            pltpu.VMEM((QUARTER, 2 * BINS), jnp.float32),
            pltpu.VMEM((2 * BINS, LAGS), jnp.bfloat16),
            pltpu.SemaphoreType.DMA((8,)),
            pltpu.VMEM((4 * ROWS, QUARTER), jnp.float32),
            pltpu.VMEM((N_COL, ROWS, 2 * BINS), jnp.bfloat16),
            pltpu.VMEM((N_ROW, ROWS, 2 * BINS), jnp.bfloat16),
            pltpu.VMEM((12, ROWS, 128), jnp.float32),
            pltpu.VMEM((6, SEG * SECOND, 128), jnp.float32),
            pltpu.VMEM((4 * PAIRS, 2 * BINS), jnp.bfloat16),
            pltpu.VMEM((4 * PAIRS, 2 * BINS), jnp.bfloat16),
            pltpu.SemaphoreType.DMA((N_COL,)),
            pltpu.SemaphoreType.DMA((N_COL,)),
            pltpu.SemaphoreType.DMA((N_ROW,)),
            pltpu.SemaphoreType.DMA((N_ROW,)),
        ],
        compiler_params=pltpu.CompilerParams(collective_id=0, has_side_effects=True, vmem_limit_bytes=16 << 20),
        name="stack",
    )(
        *(
            pltpu.with_memory_space_constraint(operand, pltpu.HBM)
            for operand in (
                offsets, band_lo, band_hi, live, traces,
                jnp.asarray(taper_table()), jnp.asarray(dft_table()), jnp.asarray(lag_table(), jnp.bfloat16),
            )
        )
    )
    return stacked


def solution(mesh):
    in_specs = (
        P(("row", "col"), None),
        P(("row", "col"), None),
        P(("row", "col")),
        P(("row", "col")),
        P(("row", "col")),
    )
    out_specs = P("row", "col", None, None, None)
    return jax.shard_map(body, mesh=mesh, in_specs=in_specs, out_specs=out_specs, check_vma=False)
```

```python
import functools
import math

import jax
import jax.numpy as jnp
import numpy as np
from jax import lax
from jax.experimental import pallas as pl
from jax.experimental.pallas import tpu as pltpu
from jax.sharding import PartitionSpec as P

SEG = 8
SAMPLES = 1024
QUARTER = SAMPLES // 4
BINS = 256
LAGS = 512
TRACE = 4096
CH_DEV = 2
ROWS = CH_DEV * SEG
MESH = pl.DeviceIdType.MESH

NZ, NY = 16, 4
N_ROW, N_COL = 16, 32
PANEL = N_COL * CH_DEV
SECOND = N_ROW * CH_DEV
PAIRS = CH_DEV * SECOND

GROUPS = (
    ((0, 0), (1, 0), (-1, 0), (0, 1)),
    ((2, 0), (-2, 0), (1, 1), (-1, 1)),
    ((2, 1), (-2, 1), (5, 0), (-5, 0)),
    ((4, 0), (6, 0), (-4, 0), (-6, 0)),
    ((3, 0), (-3, 0), (7, 0), (-7, 0)),
    ((5, 1), (-5, 1), (4, 1), (6, 1)),
    ((-4, 1), (-6, 1), (8, 0), (3, 1)),
    ((-3, 1), (7, 1), (-7, 1), (8, 1)),
)
PLACES = tuple(d for group in GROUPS for d in group)
SLOT = {d: n for n, d in enumerate(PLACES)}
FAR = ((5, 0), (-5, 0))
NEAR = ((1, 0), (-1, 0), (2, 0), (-2, 0), (0, 1), (1, 1), (-1, 1), (2, 1), (-2, 1))
RELAYS = {(5, 0): NEAR[:4] + ((3, 0),) + NEAR[4:] + ((3, 1),), (-5, 0): NEAR}
COL_STEPS = FAR + NEAR + ((3, 0), (3, 1))
ROW_STEPS = tuple(
    (dy, dx, dc) for dy in (2, 1, -1, 0) for dx in (1, 0) for dc in (0, 1) if (dy, dx, dc) != (0, 0, 0)
)


def dft_table():
    times = np.arange(QUARTER)
    freqs = np.arange(BINS) + 1
    phase = (times[:, None] * freqs[None, :] % SAMPLES) * (2.0 * math.pi / SAMPLES)
    return np.concatenate([np.cos(phase), -np.sin(phase)], axis=1).astype(np.float32)


def taper_table():
    times = np.arange(SAMPLES)
    return (0.5 - 0.5 * np.cos(times * (2.0 * math.pi / SAMPLES))).reshape(4, QUARTER).astype(np.float32)


def lag_table():
    freqs = np.arange(BINS) + 1
    shifts = np.arange(LAGS) - LAGS // 2
    phase = np.mod(freqs[:, None] * shifts[None, :], SAMPLES) * (2.0 * math.pi / SAMPLES)
    return np.concatenate([np.cos(phase), -np.sin(phase)], axis=0).astype(np.float32)


def col_device(step, sign=1):
    col = lax.axis_index("col")
    z = lax.rem(col // 2 + sign * step[0] + 2 * NZ, NZ)
    x = lax.rem(col % 2 + step[1], 2)
    return {"col": z * 2 + x}


def row_device(step, sign=1):
    row = lax.axis_index("row")
    y = lax.rem(row // 4 + sign * step[0] + NY, NY)
    x = lax.rem((row // 2) % 2 + step[1], 2)
    core = lax.rem(row % 2 + step[2], 2)
    return {"row": (y * 2 + x) * 2 + core}


def whiten(traces, offsets, band_lo, band_hi, live, taper, dft, pieces, dft_load):
    sub = lax.broadcasted_iota(jnp.int32, (SEG, BINS), 0)
    for k in range(CH_DEV):
        start = jnp.zeros((SEG, BINS), jnp.int32)
        for s in range(SEG):
            start = jnp.where(sub == s, offsets[k, s], start)
        cut = [jnp.zeros((SEG, QUARTER), jnp.float32) for _ in range(4)]
        for block in range(TRACE // QUARTER):
            samples = jnp.broadcast_to(
                traces[k : k + 1, block * QUARTER : (block + 1) * QUARTER], (SEG, QUARTER)
            )
            for q in range(4):
                place = block - q
                if 0 <= place <= TRACE // QUARTER - 4:
                    cut[q] = jnp.where(start == place * QUARTER, samples, cut[q])
        for q in range(4):
            row = q * ROWS + k * SEG
            pieces[row : row + SEG, :] = cut[q] * taper[q : q + 1, :]
    dft_load.wait()
    parts = jnp.dot(
        pieces[...], dft[...], precision=lax.Precision.HIGHEST, preferred_element_type=jnp.float32
    )
    lane = lax.broadcasted_iota(jnp.int32, (ROWS, BINS), 1)
    spec_re = parts[:ROWS, :BINS]
    spec_im = parts[:ROWS, BINS:]
    for q in range(1, 4):
        part_re = parts[q * ROWS : (q + 1) * ROWS, :BINS]
        part_im = parts[q * ROWS : (q + 1) * ROWS, BINS:]
        turn = ((lane + 1) * q) & 3
        spec_re = spec_re + jnp.where(
            turn == 0, part_re, jnp.where(turn == 1, part_im, jnp.where(turn == 2, -part_re, -part_im))
        )
        spec_im = spec_im + jnp.where(
            turn == 0, part_im, jnp.where(turn == 1, -part_re, jnp.where(turn == 2, -part_im, part_re))
        )
    amp = jnp.sqrt(spec_re * spec_re + spec_im * spec_im)

    def moved(by):
        return jnp.where((lane >= by) & (lane < BINS + by), pltpu.roll(amp, by % BINS, 1), 0.0)

    smooth = (moved(2) + moved(1) + amp + moved(-1) + moved(-2)) / 5.0
    level = jnp.sum(amp, axis=1, keepdims=True) * (1.0 / BINS)
    factor = 1.0 / (smooth + 0.1 * level + 1e-06)
    first = lax.broadcasted_iota(jnp.int32, (ROWS, BINS), 0) < SEG
    low = jnp.where(first, band_lo[0], band_lo[1])
    high = jnp.where(first, band_hi[0], band_hi[1])
    alive = jnp.where(first, live[0], live[1])
    inside = (lane >= low) & (lane < high) & (alive == 1)
    factor = factor * jnp.where(inside, 1.0, 0.0)
    return jnp.concatenate([spec_re * factor, spec_im * factor], axis=1).astype(jnp.bfloat16)


def kernel(
    offsets_in, band_lo_in, band_hi_in, live_in, traces_in, taper_in, dft_in, lags_in, out,
    offsets, band_lo, band_hi, live, traces, taper, dft, lags, load_sem, pieces, firsts, seconds, first_f32, second_mix, cross_a, cross_b,
    first_send, first_recv, second_send, second_recv,
):
    loads = [
        pltpu.make_async_copy(source, target, load_sem.at[n])
        for n, (source, target) in enumerate(
            (
                (traces_in, traces), (offsets_in, offsets), (band_lo_in, band_lo), (band_hi_in, band_hi),
                (live_in, live), (taper_in, taper), (dft_in, dft), (lags_in, lags),
            )
        )
    ]
    for load in loads:
        load.start()
    barrier = pltpu.get_barrier_semaphore()
    for step in COL_STEPS:
        pl.semaphore_signal(barrier, inc=1, device_id=col_device(step, -1), device_id_type=MESH)
    for step in ROW_STEPS:
        pl.semaphore_signal(barrier, inc=1, device_id=row_device(step, -1), device_id_type=MESH)

    for load in loads[:-2]:
        load.wait()
    white = whiten(traces, offsets, band_lo, band_hi, live, taper, dft, pieces, loads[-2])
    my_row = lax.axis_index("row")
    firsts[0] = white
    seconds[my_row] = white
    pl.semaphore_wait(barrier, len(COL_STEPS) + len(ROW_STEPS))

    def first_copy(held, step):
        slot = SLOT[(held[0] + step[0], (held[1] + step[1]) % 2)]
        return pltpu.make_async_remote_copy(
            src_ref=firsts.at[SLOT[held]],
            dst_ref=firsts.at[slot],
            send_sem=first_send.at[slot],
            recv_sem=first_recv.at[slot],
            device_id=col_device(step),
            device_id_type=MESH,
        )

    copies = {}
    for step in FAR + NEAR:
        copies[step] = first_copy((0, 0), step)
    second_copies = []
    for n, step in enumerate(ROW_STEPS):
        second_copies.append(
            pltpu.make_async_remote_copy(
                src_ref=firsts.at[0],
                dst_ref=seconds.at[my_row],
                send_sem=second_send.at[n],
                recv_sem=second_recv.at[n],
                device_id=row_device(step),
                device_id_type=MESH,
            )
        )
    for step in FAR:
        copies[step].start()
    for copy in second_copies:
        copy.start()
    for step in NEAR:
        copies[step].start()

    arrived = {(0, 0)}

    def take(place):
        if place not in arrived:
            arrived.add(place)
            copies[place].wait_recv()

    for place, steps in RELAYS.items():
        take(place)
        for step in steps:
            copy = first_copy(place, step)
            copies[(place[0] + step[0], (place[1] + step[1]) % 2)] = copy
            copy.start()

    def mix(row):
        block = seconds[row].astype(jnp.float32) * (1.0 / math.sqrt(SEG * BINS))
        for k in range(CH_DEV):
            for tile in range(2):
                re = block[k * SEG : k * SEG + SEG, tile * 128 : tile * 128 + 128]
                im = block[k * SEG : k * SEG + SEG, BINS + tile * 128 : BINS + tile * 128 + 128]
                at = pl.ds(row * 2 + k, SEG, stride=SECOND)
                for m, mixed in enumerate((re, re - im, re + im)):
                    second_mix[2 * m + tile, at, :] = mixed

    mix(my_row)
    for n in range(len(ROW_STEPS) - 1, -1, -1):
        second_copies[n].wait_recv()
        mix(row_device(ROW_STEPS[n], -1)["row"])

    loads[-1].wait()
    my_col = lax.axis_index("col")

    def source_of(place):
        return lax.rem(my_col // 2 - place[0] + 2 * NZ, NZ) * 2 + lax.rem(my_col % 2 + place[1], 2)

    crosses = (cross_a, cross_b)

    def cross_block(n, v, buffer, base):
        block = firsts[n].astype(jnp.float32)
        for tile in range(4):
            first_f32[6 * v + tile] = block[:, tile * 128 : tile * 128 + 128]
        for tile in range(2):
            lo = tile * 128
            first_f32[6 * v + 4 + tile] = block[:, lo : lo + 128] + block[:, BINS + lo : BINS + lo + 128]
        for half in range(2):
            lo = half * 128
            total = [[[None] * 4 for _ in range(3)] for _ in range(CH_DEV)]
            for s in range(SEG):
                b = [
                    [second_mix[2 * m + half, s * SECOND + jt * 8 : s * SECOND + jt * 8 + 8, :] for jt in range(4)]
                    for m in range(3)
                ]
                for k in range(CH_DEV):
                    row = k * SEG + s
                    a = [first_f32[6 * v + tile + half, pl.ds(row, 8, stride=0), :] for tile in (4, 2, 0)]
                    for m in range(3):
                        for jt in range(4):
                            term = a[m] * b[m][jt]
                            old = total[k][m][jt]
                            total[k][m][jt] = term if old is None else old + term
            for k in range(CH_DEV):
                for pair in range(2):
                    tiles = (2 * pair, 2 * pair + 1)
                    re = [total[k][0][jt] - total[k][1][jt] for jt in tiles]
                    im = [total[k][0][jt] - total[k][2][jt] for jt in tiles]
                    at = pl.ds(pl.multiple_of(base + k * SECOND + pair * 16, 16), 16)
                    buffer[at, lo : lo + 128] = jnp.concatenate(re, 0).astype(jnp.bfloat16)
                    buffer[at, BINS + lo : BINS + lo + 128] = jnp.concatenate(im, 0).astype(jnp.bfloat16)

    def lag_half(g, u):
        at = pl.ds(pl.multiple_of(u * 256, 256), 256)
        corr = jnp.dot(crosses[g % 2][...], lags[:, at], preferred_element_type=jnp.float32)
        corr = corr.astype(jnp.bfloat16)
        for t, place in enumerate(GROUPS[g]):
            rows = corr[t * PAIRS : (t + 1) * PAIRS].reshape(CH_DEV, N_ROW, CH_DEV, 256)
            out[pl.ds(source_of(place) * 2, 2), 0, :, :, at] = rows

    def step(g, u):
        if g > 0:
            lag_half(g - 1, u)
        for v in range(2):
            t = 2 * u + v
            cross_block(g * 4 + t, v, crosses[g % 2], t * PAIRS)

    for g, group in enumerate(GROUPS):
        if g < len(GROUPS) - 2:
            for place in group:
                take(place)

            @pl.loop(0, 2)
            def _(u):
                step(g, u)
        else:
            for u in range(2):
                take(group[2 * u])
                take(group[2 * u + 1])
                step(g, u)
    for u in range(2):
        lag_half(len(GROUPS) - 1, u)

    for copy in copies.values():
        copy.wait_send()
    for copy in second_copies:
        copy.wait_send()


def body(traces, offsets, band_lo, band_hi, live):
    vmem = pl.BlockSpec(memory_space=pltpu.VMEM)
    hbm = pl.BlockSpec(memory_space=pltpu.HBM)
    stacked = pl.pallas_call(
        kernel,
        out_shape=jax.ShapeDtypeStruct((PANEL, 1, N_ROW, CH_DEV, LAGS), jnp.bfloat16),
        in_specs=[hbm] * 8,
        out_specs=vmem,
        scratch_shapes=[
            pltpu.SMEM((CH_DEV, SEG), jnp.int32),
            pltpu.SMEM((CH_DEV,), jnp.int32),
            pltpu.SMEM((CH_DEV,), jnp.int32),
            pltpu.SMEM((CH_DEV,), jnp.int32),
            pltpu.VMEM((CH_DEV, TRACE), jnp.float32),
            pltpu.VMEM((4, QUARTER), jnp.float32),
            pltpu.VMEM((QUARTER, 2 * BINS), jnp.float32),
            pltpu.VMEM((2 * BINS, LAGS), jnp.bfloat16),
            pltpu.SemaphoreType.DMA((8,)),
            pltpu.VMEM((4 * ROWS, QUARTER), jnp.float32),
            pltpu.VMEM((N_COL, ROWS, 2 * BINS), jnp.bfloat16),
            pltpu.VMEM((N_ROW, ROWS, 2 * BINS), jnp.bfloat16),
            pltpu.VMEM((12, ROWS, 128), jnp.float32),
            pltpu.VMEM((6, SEG * SECOND, 128), jnp.float32),
            pltpu.VMEM((4 * PAIRS, 2 * BINS), jnp.bfloat16),
            pltpu.VMEM((4 * PAIRS, 2 * BINS), jnp.bfloat16),
            pltpu.SemaphoreType.DMA((N_COL,)),
            pltpu.SemaphoreType.DMA((N_COL,)),
            pltpu.SemaphoreType.DMA((N_ROW,)),
            pltpu.SemaphoreType.DMA((N_ROW,)),
        ],
        compiler_params=pltpu.CompilerParams(collective_id=0, has_side_effects=True, vmem_limit_bytes=16 << 20),
        name="stack",
    )(
        *(
            pltpu.with_memory_space_constraint(operand, pltpu.HBM)
            for operand in (
                offsets, band_lo, band_hi, live, traces,
                jnp.asarray(taper_table()), jnp.asarray(dft_table()), jnp.asarray(lag_table(), jnp.bfloat16),
            )
        )
    )
    return stacked


def solution(mesh):
    in_specs = (
        P(("row", "col"), None),
        P(("row", "col"), None),
        P(("row", "col")),
        P(("row", "col")),
        P(("row", "col")),
    )
    out_specs = P("row", "col", None, None, None)
    return jax.shard_map(body, mesh=mesh, in_specs=in_specs, out_specs=out_specs, check_vma=False)
```
